256 devices in a mesh: seq: 32 (over z, y), tp: 8 (over x, core).
Axes of the slice: x: 4, y: 4, z: 8, core: 2. Of those that a mesh axis runs over, the one named last changes fastest.
Arguments:
- gate: bfloat16 [8192, 8192], P('seq', 'tp'), may hold values from -6 to 6
- conv_input: bfloat16 [8192, 8192], P('seq', 'tp'), may hold values from -6 to 6
- filters: bfloat16 [512, 128], P('tp'), may hold values from -0.5 to 0.5
- out_weight: bfloat16 [4096, 8192], P('seq', 'tp'), may hold values from -0.0625 to 0.0625
- upstream: bfloat16 [8192, 4096], P('seq', 'tp'), may hold values from -12 to 12
Outputs:
- grad_gate: bfloat16 [8192, 8192], P('seq', 'tp')
- grad_input: bfloat16 [8192, 8192], P('seq', 'tp')
- grad_filter: float32 [512, 128], P('tp')
- grad_weight: bfloat16 [4096, 8192], P('seq', 'tp')
The draws below stay inside these ranges and needn't reach their ends.
All inputs are finite; a program needn't handle non-finite values.
Results may differ from the reference program's by a relative error of at most 0.018.
Values may be sent and summed in bfloat16 or wider, within the bound.
No kernel may reach another device: no remote copies, remote signals or barrier semaphores. Data moves between devices by JAX's collectives and lax.ppermute only.
A program may use at most 128 MiB of HBM per device.

```python
import jax
import jax.numpy as jnp
from jax import lax

D = 8192
E = 4096
K = 128
GROUP = 16
TOK_DEV = 256
TOKENS = 8192
GROUPS = 512
N_SEQ = 32


def with_spikes(entries, key, source, target, blocks, factor):
    owner, partner = [(jnp.arange(entries.shape[dim]) // (entries.shape[dim] // blocks)).reshape([-1 if axis == dim else 1 for axis in range(entries.ndim)]) for dim in (source, target)]
    chosen = jax.random.permutation(key, blocks)[partner]
    strong = (owner == chosen) | (owner == (partner + blocks // 2) % blocks)
    return jnp.where(strong, factor * entries, entries)


def block_levels(rng, extent, shards, smallest, high):
    factor_of, own = 1.0, jax.random.fold_in(rng, 6)
    for axis_at, parts in shards:
        draws = jnp.exp(jax.random.uniform(jax.random.fold_in(own, axis_at), (parts,), jnp.float32, smallest / len(shards), high / len(shards)))
        factor_of = factor_of * jnp.repeat(draws, extent[axis_at] // parts).reshape([-1 if axis == axis_at else 1 for axis in range(len(extent))])
    return factor_of


def bell_draw(rng, shape, scale, most, pieces=(), kind=jnp.bfloat16):
    drawn = scale * jax.random.normal(rng, shape, jnp.float32)
    if pieces:
        drawn = drawn * block_levels(rng, shape, pieces, -0.22, 0.18)
    return jnp.clip(drawn, -most, most).astype(kind)


def bell_draw_with(key, dims, width, limit, pieces, heavy, dtype=jnp.bfloat16):
    result = width * jax.random.normal(key, dims, jnp.float32)
    if pieces:
        result = result * block_levels(key, dims, pieces, -0.22, 0.18)
    return jnp.clip(with_spikes(result, jax.random.fold_in(key, 3), *heavy), -limit, limit).astype(dtype)


def setup_inputs(seed: int = 0) -> dict:
    streams_of = jax.random.split(jax.random.key(seed), 6)
    gate = bell_draw(streams_of[0], (TOKENS, D), 1.0, 6.0, ((0, 32), (1, 8)))
    conv_input = bell_draw(streams_of[1], (TOKENS, D), 1.0, 6.0, ((0, 32), (1, 8)))
    filters = bell_draw(streams_of[2], (GROUPS, K), K ** -0.5, 0.5, ((0, 8),))
    out_weight = bell_draw(streams_of[3], (E, D), D ** -0.5, 0.0625, ((0, 32), (1, 8)))
    upstream = bell_draw_with(streams_of[4], (TOKENS, E), 1.0, 12.0, ((0, 32), (1, 8)), (0, 1, 32, 2.75))
    return {"gate": gate, "conv_input": conv_input, "filters": filters, "out_weight": out_weight, "upstream": upstream}


def skewed(source_table):
    row_count = source_table.shape[-2]
    leading = source_table.shape[:-2]
    flattened = source_table.reshape(leading + (2 * row_count * row_count,))
    flattened = jnp.pad(flattened, [(0, 0)] * len(leading) + [(0, row_count)])
    return flattened.reshape(leading + (row_count, 2 * row_count + 1))[..., : row_count + 1]


def toeplitz(filters):
    tap_count = filters.shape[-1]
    zero_pad = jnp.zeros_like(filters)

    def banded(source):
        reverse = source[:, ::-1]
        source_table = jnp.broadcast_to(reverse[:, None, :], (source.shape[0], tap_count, 2 * tap_count))
        return skewed(source_table)[:, ::-1, :tap_count]

    lower_band = banded(jnp.concatenate([zero_pad, filters], axis=-1))
    upper_band = banded(jnp.concatenate([filters, zero_pad], axis=-1))
    return lower_band, upper_band


def diagonal_sums(lower_part, upper_part):
    tap_count = lower_part.shape[-1]
    row_index = jnp.arange(tap_count)[:, None]
    col_index = jnp.arange(tap_count)[None, :]
    merged = jnp.where(row_index >= col_index, lower_part, upper_part)
    doubled = jnp.concatenate([merged, merged], axis=-1)
    return jnp.sum(skewed(doubled)[:, :, 1:][:, :, ::-1], axis=1)


def reference(gate, conv_input, filters, out_weight, upstream):
    tap_count = filters.shape[1]
    highest = lax.Precision.HIGHEST
    lower_band, upper_band = toeplitz(filters)
    lower_wide = lower_band.astype(jnp.float32)
    upper_wide = upper_band.astype(jnp.float32)
    block_count = TOKENS // tap_count
    input_blocks = conv_input.astype(jnp.float32).reshape(block_count, tap_count, GROUPS, GROUP)
    prior_blocks = jnp.concatenate([jnp.zeros_like(input_blocks[:1]), input_blocks[:-1]], axis=0)
    conv_out = jnp.einsum("gim,bmgc->bigc", lower_wide, input_blocks, precision=highest)
    conv_out = conv_out + jnp.einsum("gim,bmgc->bigc", upper_wide, prior_blocks, precision=highest)
    conv_out = conv_out.reshape(TOKENS, D)
    gate_wide = gate.astype(jnp.float32)
    mixed = (gate_wide * conv_out).astype(jnp.bfloat16)
    d_out = jnp.dot(upstream, out_weight, preferred_element_type=jnp.float32)
    grad_gate = (d_out * conv_out).astype(jnp.bfloat16)
    d_conv = (d_out * gate_wide).astype(jnp.bfloat16)
    conv_blocks = d_conv.astype(jnp.float32).reshape(block_count, tap_count, GROUPS, GROUP)
    next_blocks = jnp.concatenate([conv_blocks[1:], jnp.zeros_like(conv_blocks[:1])], axis=0)
    grad_input = jnp.einsum("gim,bigc->bmgc", lower_wide, conv_blocks, precision=highest)
    grad_input = grad_input + jnp.einsum("gim,bigc->bmgc", upper_wide, next_blocks, precision=highest)
    grad_input = grad_input.reshape(TOKENS, D).astype(jnp.bfloat16)
    factor = TOKENS ** -0.5
    lower_part = jnp.einsum("bigc,bmgc->gim", conv_blocks, input_blocks, precision=highest)
    upper_part = jnp.einsum("bigc,bmgc->gim", conv_blocks, prior_blocks, precision=highest)
    grad_filter = diagonal_sums(lower_part, upper_part) * factor
    upstream_runs = upstream.reshape(N_SEQ, TOK_DEV, E)
    mixed_runs = mixed.reshape(N_SEQ, TOK_DEV, D)

    def add_run(summed, pair):
        upstream_run, mixed_run = pair
        partial_sum = lax.dot_general(upstream_run, mixed_run, (((0,), (0,)), ((), ())), preferred_element_type=jnp.float32)
        rounded = lax.optimization_barrier(partial_sum.astype(jnp.bfloat16))
        return summed + rounded.astype(jnp.float32), None

    summed, unused = lax.scan(add_run, jnp.zeros((E, D), jnp.float32), (upstream_runs, mixed_runs))
    grad_weight = (summed * factor).astype(jnp.bfloat16)
    return grad_gate, grad_input, grad_filter, grad_weight
```

```python
import jax
import jax.numpy as jnp
from jax import lax
from jax.experimental import pallas as pl
from jax.experimental.pallas import tpu as pltpu
from jax.sharding import Mesh
from jax.sharding import PartitionSpec as P

GROUP = 16
TAPS = 128
LANES = 128
F32 = jnp.float32
BF16 = jnp.bfloat16
SIZES = {"z": 8, "y": 4, "x": 4, "c": 2}
SEQ = ("z", "y")
TP = ("x", "c")


def shift(block, axis, distance):
    size = SIZES[axis]
    return lax.ppermute(block, axis, [(i, (i + distance) % size) for i in range(size)])


def from_behind(block, distance):
    devices = range(SIZES["z"] * SIZES["y"])
    route = [(i - distance, i) for i in devices if i - distance in devices]
    return lax.ppermute(block, SEQ, route)


def split_features_kernel(u_ref, *outs):
    y = lax.axis_index("y")
    for d, out in enumerate(outs):
        start = pl.multiple_of(lax.rem(y + d, 4) * LANES, LANES)
        out[...] = u_ref[:, pl.ds(start, LANES)]


def split_features(u):
    shape = jax.ShapeDtypeStruct((u.shape[0], LANES), u.dtype)
    return pl.pallas_call(
        split_features_kernel, out_shape=[shape] * 4, name="split_features"
    )(u)


def rows_and_cols():
    row = lax.broadcasted_iota(jnp.int32, (TAPS, TAPS), 0)
    col = lax.broadcasted_iota(jnp.int32, (TAPS, TAPS), 1)
    return row, col


def lane_group(shape):
    return lax.broadcasted_iota(jnp.int32, shape, len(shape) - 1) % LANES // GROUP


def pick_groups(stacked):
    lanes = lane_group((TAPS, 2 * LANES))
    out = stacked[:TAPS]
    for g in range(1, LANES // GROUP):
        out = jnp.where(lanes == g, stacked[g * TAPS : (g + 1) * TAPS], out)
    return out


def conv_kernel(prev_ref, x_ref, gate_ref, rev_ref, mixed_ref, out_ref):
    row, col = rows_and_cols()
    bands = []
    for g in range(LANES // GROUP):
        taps = jnp.broadcast_to(rev_ref[pl.ds(g, 1), :].astype(F32), (TAPS, TAPS))
        ring = pltpu.roll(taps, 1, 1, stride=1, stride_axis=0)
        upper = jnp.where(col > row, ring, 0.0)
        lower = jnp.where(col <= row, ring, 0.0)
        bands.append(jnp.concatenate([upper, lower], axis=1).astype(BF16))
    band = jnp.concatenate(bands, axis=0)
    x0, x1 = x_ref[:TAPS], x_ref[TAPS:]
    first = jnp.concatenate([prev_ref[...], x0], axis=0)
    second = jnp.concatenate([x0, x1], axis=0)
    window = jnp.concatenate([first, second], axis=1)
    conv = pick_groups(jnp.dot(band, window, preferred_element_type=F32))
    conv = jnp.concatenate([conv[:, :LANES], conv[:, LANES:]], axis=0)
    out_ref[...] = conv
    mixed_ref[...] = (gate_ref[...].astype(F32) * conv).astype(BF16)


def tile(rows):
    return pl.BlockSpec((rows, LANES), lambda i: (0, i))


def taps_tile():
    return pl.BlockSpec((LANES // GROUP, TAPS), lambda i: (i, 0))


def conv_forward(prev, x, gate, rev):
    rows, channels = x.shape
    return pl.pallas_call(
        conv_kernel,
        grid=(channels // LANES,),
        in_specs=[tile(TAPS), tile(rows), tile(rows), taps_tile()],
        out_specs=[tile(rows), tile(rows)],
        out_shape=[
            jax.ShapeDtypeStruct(x.shape, BF16),
            jax.ShapeDtypeStruct(x.shape, F32),
        ],
        name="conv_forward",
    )(prev, x, gate, rev)


def back_kernel(d_ref, next_ref, taps_ref, out_ref):
    row, col = rows_and_cols()
    bands = []
    for g in range(LANES // GROUP):
        taps = jnp.broadcast_to(taps_ref[pl.ds(g, 1), :].astype(F32), (TAPS, TAPS))
        ring = pltpu.roll(taps, 0, 1, stride=1, stride_axis=0)
        lower = jnp.where(col >= row, ring, 0.0)
        upper = jnp.where(col < row, ring, 0.0)
        bands.append(jnp.concatenate([lower, upper], axis=1).astype(BF16))
    band = jnp.concatenate(bands, axis=0)
    d0, d1 = d_ref[:TAPS], d_ref[TAPS:]
    first = jnp.concatenate([d0, d1], axis=0)
    second = jnp.concatenate([d1, next_ref[...]], axis=0)
    window = jnp.concatenate([first, second], axis=1)
    conv = pick_groups(jnp.dot(band, window, preferred_element_type=F32))
    out_ref[:TAPS] = conv[:, :LANES].astype(BF16)
    out_ref[TAPS:] = conv[:, LANES:].astype(BF16)


def conv_backward(d_conv, following, filters):
    rows, channels = d_conv.shape
    return pl.pallas_call(
        back_kernel,
        grid=(channels // LANES,),
        in_specs=[tile(rows), tile(TAPS), taps_tile()],
        out_specs=tile(rows),
        out_shape=jax.ShapeDtypeStruct(d_conv.shape, BF16),
        name="conv_backward",
    )(d_conv, following, filters)


def filter_kernel(prev_ref, x_ref, d_ref, out_ref):
    row, col = rows_and_cols()
    flip = jnp.where(row + col == TAPS - 1, 1.0, 0.0).astype(BF16)

    def flipped(block):
        return jnp.dot(flip, block, preferred_element_type=F32).astype(BF16)

    prev, x0, x1 = flipped(prev_ref[...]), flipped(x_ref[:TAPS]), flipped(x_ref[TAPS:])
    first = jnp.concatenate([prev, x0], axis=0)
    second = jnp.concatenate([x0, x1], axis=0)
    window = jnp.concatenate([first, second], axis=1)
    both = jnp.concatenate([d_ref[:TAPS], d_ref[TAPS:]], axis=1)
    lanes = lane_group(both.shape)
    zero = jnp.zeros_like(both)
    left = [jnp.where(lanes == g, both, zero) for g in range(LANES // GROUP)]
    left = jnp.concatenate(left, axis=0)
    table = lax.dot_general(
        left, window, (((1,), (1,)), ((), ())), preferred_element_type=F32
    )
    keep = col + row >= TAPS - 1
    sums = []
    for g in range(LANES // GROUP):
        part = table[g * TAPS : (g + 1) * TAPS]
        ring = jnp.where(keep, part[:, TAPS:], part[:, :TAPS])
        ring = pltpu.roll(ring, 1, 1, stride=1, stride_axis=0)
        sums.append(jnp.sum(ring, axis=0, keepdims=True))
    out_ref[...] = jnp.concatenate(sums, axis=0)


def filter_gradient(prev, x, d_conv):
    rows, channels = x.shape
    return pl.pallas_call(
        filter_kernel,
        grid=(channels // LANES,),
        in_specs=[tile(TAPS), tile(rows), tile(rows)],
        out_specs=taps_tile(),
        out_shape=jax.ShapeDtypeStruct((channels // GROUP, TAPS), F32),
        name="filter_gradient",
    )(prev, x, d_conv)


ANY = pl.BlockSpec(memory_space=pl.ANY)


def place_features(pieces, scratch):
    x, c = lax.axis_index("x"), lax.axis_index("c")
    out = []
    for at, piece in enumerate(pieces):
        k, other = at % 4, at // 4
        owner_c = c if other == 0 else 1 - c
        owner = 2 * lax.rem(x - k + 4, 4) + owner_c
        start = pl.multiple_of(owner * LANES, LANES)
        out.append((piece, scratch.at[:, pl.ds(start, LANES)]))
    return out


def run_copies(pairs, sems):
    copies = [
        pltpu.make_async_copy(source, target, sems.at[at])
        for at, (source, target) in enumerate(pairs)
    ]
    for copy in copies:
        copy.start()
    for copy in copies:
        copy.wait()


def output_kernel(*refs):
    u_refs, w_refs, outs = refs[:8], refs[8:17], refs[17:21]
    u_all, w_all, sems = refs[21:]
    z = lax.axis_index("z")
    pairs = place_features(u_refs, u_all)
    for at, k in enumerate((0, 1, 2, 3, -1, -2, -3)):
        start = pl.multiple_of(lax.rem(z - k + 8, 8) * LANES, LANES)
        pairs.append((w_refs[at], w_all.at[pl.ds(start, LANES)]))
    far = pl.multiple_of(lax.rem(z + 4, 8) * LANES, LANES)
    half = LANES // 2
    pairs.append((w_refs[7], w_all.at[pl.ds(far, half)]))
    pairs.append((w_refs[8], w_all.at[pl.ds(pl.multiple_of(far + half, half), half)]))
    run_copies(pairs, sems)
    rows = outs[0].shape[0]
    for d, out in enumerate(outs):
        out[...] = jnp.dot(
            u_all[d * rows : (d + 1) * rows], w_all[...], preferred_element_type=F32
        ).astype(BF16)


def output_partials(features, weights):
    tokens, channels = features[0].shape[0], weights[0].shape[1]
    shape = jax.ShapeDtypeStruct((tokens // 4, channels), BF16)
    vmem = pl.BlockSpec(memory_space=pltpu.VMEM)
    return pl.pallas_call(
        output_kernel,
        in_specs=[ANY] * 17,
        out_specs=[vmem] * 4,
        out_shape=[shape] * 4,
        scratch_shapes=[
            pltpu.VMEM((tokens, 8 * LANES), BF16),
            pltpu.VMEM((8 * LANES, channels), BF16),
            pltpu.SemaphoreType.DMA((17,)),
        ],
        name="output_partials",
    )(*features, *weights)


def weight_kernel(hops, *refs):
    u_refs, m_refs, outs = refs[:8], refs[8:13], refs[13:-3]
    u_all, m_all, sems = refs[-3:]
    z = lax.axis_index("z")
    pairs = place_features(u_refs, u_all)
    rows = m_refs[0].shape[0]
    half = rows // 2
    for at, start in enumerate((0, rows, 3 * rows)):
        pairs.append((m_refs[at], m_all.at[pl.ds(start, rows)]))
    pairs.append((m_refs[3], m_all.at[pl.ds(2 * rows, half)]))
    pairs.append((m_refs[4], m_all.at[pl.ds(2 * rows + half, half)]))
    run_copies(pairs, sems)
    for out, hop in zip(outs, hops):
        start = pl.multiple_of(lax.rem(z + hop + 8, 8) * LANES, LANES)
        out[...] = lax.dot_general(
            u_all[:, pl.ds(start, LANES)],
            m_all[...],
            (((0,), (0,)), ((), ())),
            preferred_element_type=F32,
        ).astype(BF16)


def weight_partials(features, mixed, hops, name):
    tokens, channels = features[0].shape[0], mixed[0].shape[1]
    shape = jax.ShapeDtypeStruct((LANES, channels), BF16)
    vmem = pl.BlockSpec(memory_space=pltpu.VMEM)

    def kernel(*refs):
        weight_kernel(hops, *refs)

    return pl.pallas_call(
        kernel,
        in_specs=[ANY] * 13,
        out_specs=[vmem] * len(hops),
        out_shape=[shape] * len(hops),
        scratch_shapes=[
            pltpu.VMEM((tokens, 8 * LANES), BF16),
            pltpu.VMEM((tokens, channels), BF16),
            pltpu.SemaphoreType.DMA((13,)),
        ],
        name=name,
    )(*features, *mixed)


def added(*terms):
    return sum(term.astype(F32) for term in terms).astype(BF16)


def shards(gate, conv_input, filters, out_weight, upstream):
    rows, channels = conv_input.shape
    half = LANES // 2
    factor = (rows * SIZES["z"] * SIZES["y"]) ** (-0.5)

    mine = split_features(upstream)
    parts = [mine[0]] + [shift(mine[d], "y", d) for d in range(1, 4)]
    own = jnp.concatenate(parts, axis=0)
    near = [own] + [shift(own, "x", k) for k in range(1, 4)]
    features = near + [shift(piece, "c", 1) for piece in near]

    ahead, behind = out_weight, out_weight
    forward, backward = [], []
    for _ in range(3):
        ahead, behind = shift(ahead, "z", 1), shift(behind, "z", -1)
        forward.append(ahead)
        backward.append(behind)
    weights = [out_weight] + forward + backward
    weights += [shift(ahead[:half], "z", 1), shift(behind[half:], "z", -1)]

    prior = from_behind(conv_input[rows - TAPS :], 1)
    mixed, conv_out = conv_forward(prior, conv_input, gate, filters[:, ::-1])
    up, down = shift(mixed, "y", 1), shift(mixed, "y", -1)
    middle = rows // 2
    far_top, far_low = shift(up[:middle], "y", 1), shift(down[middle:], "y", -1)
    mixed_all = [mixed, up, down, far_top, far_low]

    partials = output_partials(features, weights)
    terms = [partials[0]] + [shift(partials[d], "y", -d) for d in range(1, 4)]

    (far,) = weight_partials(features, mixed_all, (4,), "weight_far")
    blocks = weight_partials(features, mixed_all, (3, -3, 2, -2, 1, -1, 0), "weight_near")
    ahead, behind = shift(far[:half], "z", 1), shift(far[half:], "z", -1)
    first, last = blocks[0], blocks[1]
    ahead = jnp.concatenate([added(first[:half], ahead), first[half:]], axis=0)
    behind = jnp.concatenate([last[:half], added(last[half:], behind)], axis=0)
    for at in (2, 4):
        ahead = added(shift(ahead, "z", 1), blocks[at])
        behind = added(shift(behind, "z", -1), blocks[at + 1])
    ahead, behind = shift(ahead, "z", 1), shift(behind, "z", -1)
    summed = sum(term.astype(F32) for term in (blocks[6], ahead, behind))
    grad_weight = (summed * factor).astype(BF16)

    d_out = sum(term.astype(F32) for term in terms)
    grad_gate = (d_out * conv_out).astype(BF16)
    d_conv = (d_out * gate.astype(F32)).astype(BF16)
    following = from_behind(d_conv[:TAPS], -1)
    local = filter_gradient(prior, conv_input, d_conv)
    copies = jnp.broadcast_to(local.astype(BF16), (32, *local.shape))
    copies = lax.all_to_all(copies, SEQ, split_axis=0, concat_axis=0, tiled=True)
    grad_filter = copies.astype(F32).sum(axis=0) * factor
    grad_input = conv_backward(d_conv, following, filters)
    return (grad_gate, grad_input, grad_filter, grad_weight)


def solution(mesh):
    finer = Mesh(mesh.devices.reshape(8, 4, 4, 2), ("z", "y", "x", "c"))
    return jax.shard_map(
        shards,
        mesh=finer,
        in_specs=(P(SEQ, TP), P(SEQ, TP), P(TP, None), P(SEQ, TP), P(SEQ, TP)),
        out_specs=(P(SEQ, TP), P(SEQ, TP), P(TP, None), P(SEQ, TP)),
        check_vma=False,
    )
```

```python
import jax
import jax.numpy as jnp
from jax import lax
from jax.experimental import pallas as pl
from jax.experimental.pallas import tpu as pltpu
from jax.sharding import Mesh
from jax.sharding import PartitionSpec as P

GROUP = 16
TAPS = 128
LANES = 128
F32 = jnp.float32
BF16 = jnp.bfloat16
SIZES = {"z": 8, "y": 4, "x": 4, "c": 2}
SEQ = ("z", "y")
GRANT = pltpu.CompilerParams(vmem_limit_bytes=20 << 20)
TP = ("x", "c")


def shift(block, axis, distance):
    size = SIZES[axis]
    route = [(i, (i + distance) % size) for i in range(size)]
    return lax.ppermute(block, axis, route)


def exchanged(blocks, axis):
    return lax.all_to_all(blocks, axis, split_axis=0, concat_axis=0, tiled=True)


def from_behind(block, distance):
    devices = range(SIZES["z"] * SIZES["y"])
    route = [(i - distance, i) for i in devices if i - distance in devices]
    return lax.ppermute(block, SEQ, route)


def rows_and_cols():
    row = lax.broadcasted_iota(jnp.int32, (TAPS, TAPS), 0)
    col = lax.broadcasted_iota(jnp.int32, (TAPS, TAPS), 1)
    return row, col


def lane_group(shape):
    return lax.broadcasted_iota(jnp.int32, shape, len(shape) - 1) % LANES // GROUP


def pick_groups(stacked):
    lanes = lane_group((TAPS, 2 * LANES))
    out = stacked[:TAPS]
    for g in range(1, LANES // GROUP):
        out = jnp.where(lanes == g, stacked[g * TAPS : (g + 1) * TAPS], out)
    return out


STEP = 512


def tiles():
    return [slice(at, at + LANES) for at in range(0, STEP, LANES)]


def group_rows(at):
    return slice(at // GROUP, (at + LANES) // GROUP)


def banded(rings, first):
    bands = []
    for ring in rings:
        left = jnp.where(first, ring, 0.0)
        right = jnp.where(first, 0.0, ring)
        bands.append(jnp.concatenate([left, right], axis=1).astype(BF16))
    return jnp.concatenate(bands, axis=0)


def rings_of(taps, turn):
    out = []
    for g in range(LANES // GROUP):
        wide = jnp.broadcast_to(taps[g : g + 1], (TAPS, TAPS))
        out.append(pltpu.roll(wide, turn, 1, stride=1, stride_axis=0))
    return out


def conv_kernel(prev_ref, x_ref, gate_ref, taps_ref, mixed_ref, out_ref):
    row, col = rows_and_cols()
    flip = jnp.where(row + col == TAPS - 1, 1.0, 0.0).astype(BF16)
    taps = jnp.dot(taps_ref[...], flip, preferred_element_type=F32)
    for at in tiles():
        band = banded(rings_of(taps[group_rows(at.start)], 1), col > row)
        x0, x1 = x_ref[:TAPS, at], x_ref[TAPS:, at]
        first = jnp.concatenate([prev_ref[:, at], x0], axis=0)
        second = jnp.concatenate([x0, x1], axis=0)
        window = jnp.concatenate([first, second], axis=1)
        conv = pick_groups(jnp.dot(band, window, preferred_element_type=F32))
        conv = jnp.concatenate([conv[:, :LANES], conv[:, LANES:]], axis=0)
        out_ref[:, at] = conv
        mixed_ref[:, at] = (gate_ref[:, at].astype(F32) * conv).astype(BF16)


def tile(rows):
    return pl.BlockSpec((rows, STEP), lambda i: (0, i))


def taps_tile():
    return pl.BlockSpec((STEP // GROUP, TAPS), lambda i: (i, 0))


def conv_forward(prev, x, gate, filters):
    rows, channels = x.shape
    return pl.pallas_call(
        conv_kernel,
        grid=(channels // STEP,),
        in_specs=[tile(TAPS), tile(rows), tile(rows), taps_tile()],
        out_specs=[tile(rows), tile(rows)],
        out_shape=[
            jax.ShapeDtypeStruct(x.shape, BF16),
            jax.ShapeDtypeStruct(x.shape, F32),
        ],
        name="conv_forward",
        compiler_params=GRANT,
    )(prev, x, gate, filters)


def back_kernel(d_ref, next_ref, taps_ref, out_ref):
    row, col = rows_and_cols()
    taps = taps_ref[...].astype(F32)
    for at in tiles():
        band = banded(rings_of(taps[group_rows(at.start)], 0), col >= row)
        d0, d1 = d_ref[:TAPS, at], d_ref[TAPS:, at]
        first = jnp.concatenate([d0, d1], axis=0)
        second = jnp.concatenate([d1, next_ref[:, at]], axis=0)
        window = jnp.concatenate([first, second], axis=1)
        conv = pick_groups(jnp.dot(band, window, preferred_element_type=F32))
        out_ref[:TAPS, at] = conv[:, :LANES].astype(BF16)
        out_ref[TAPS:, at] = conv[:, LANES:].astype(BF16)


def conv_backward(d_conv, following, filters):
    rows, channels = d_conv.shape
    return pl.pallas_call(
        back_kernel,
        grid=(channels // STEP,),
        in_specs=[tile(rows), tile(TAPS), taps_tile()],
        out_specs=tile(rows),
        out_shape=jax.ShapeDtypeStruct(d_conv.shape, BF16),
        name="conv_backward",
        compiler_params=GRANT,
    )(d_conv, following, filters)


def gradient_kernel(*refs):
    terms, (conv_ref, gate_ref, prev_ref, x_ref) = refs[:4], refs[4:8]
    grad_gate_ref, d_ref, head_ref, out_ref = refs[8:]
    row, col = rows_and_cols()
    flip = jnp.where(row + col == TAPS - 1, 1.0, 0.0).astype(BF16)
    keep = col + row >= TAPS - 1

    def flipped(block):
        return jnp.dot(flip, block, preferred_element_type=F32).astype(BF16)

    prev, x0, x1 = flipped(prev_ref[...]), flipped(x_ref[:TAPS]), flipped(x_ref[TAPS:])
    for at in tiles():
        d_out = sum(term[:, at].astype(F32) for term in terms)
        grad_gate_ref[:, at] = (d_out * conv_ref[:, at]).astype(BF16)
        d_conv = (d_out * gate_ref[:, at].astype(F32)).astype(BF16)
        d_ref[:, at] = d_conv
        head_ref[:, at] = d_conv[:TAPS]
        first = jnp.concatenate([prev[:, at], x0[:, at]], axis=0)
        second = jnp.concatenate([x0[:, at], x1[:, at]], axis=0)
        window = jnp.concatenate([first, second], axis=1)
        both = jnp.concatenate([d_conv[:TAPS], d_conv[TAPS:]], axis=1)
        lanes = lane_group(both.shape)
        zero = jnp.zeros_like(both)
        left = [jnp.where(lanes == g, both, zero) for g in range(LANES // GROUP)]
        left = jnp.concatenate(left, axis=0)
        table = lax.dot_general(
            left, window, (((1,), (1,)), ((), ())), preferred_element_type=F32
        )
        sums = []
        for g in range(LANES // GROUP):
            part = table[g * TAPS : (g + 1) * TAPS]
            ring = jnp.where(keep, part[:, TAPS:], part[:, :TAPS])
            ring = pltpu.roll(ring, 1, 1, stride=1, stride_axis=0)
            sums.append(jnp.sum(ring, axis=0, keepdims=True))
        out_ref[group_rows(at.start)] = jnp.concatenate(sums, axis=0)


def output_gradients(terms, conv_out, gate, prev, x):
    rows, channels = x.shape
    return pl.pallas_call(
        gradient_kernel,
        grid=(channels // STEP,),
        in_specs=[tile(rows)] * 6 + [tile(TAPS), tile(rows)],
        out_specs=[tile(rows), tile(rows), tile(TAPS), taps_tile()],
        out_shape=[
            jax.ShapeDtypeStruct(x.shape, BF16),
            jax.ShapeDtypeStruct(x.shape, BF16),
            jax.ShapeDtypeStruct(prev.shape, BF16),
            jax.ShapeDtypeStruct((channels // GROUP, TAPS), F32),
        ],
        name="output_gradients",
        compiler_params=GRANT,
    )(*terms, conv_out, gate, prev, x)


ANY = pl.BlockSpec(memory_space=pl.ANY)
VMEM = pl.BlockSpec(memory_space=pltpu.VMEM)


def on_chip(block):
    return pltpu.with_memory_space_constraint(block, pltpu.VMEM)


def place_features(pieces, scratch):
    x, c = lax.axis_index("x"), lax.axis_index("c")
    out = []
    for at, piece in enumerate(pieces):
        owner_c = c if at < 4 else 1 - c
        owner = 2 * lax.rem(x - at % 4 + 4, 4) + owner_c
        start = pl.multiple_of(owner * LANES, LANES)
        out.append((piece, scratch.at[:, pl.ds(start, LANES)]))
    return out


def run_copies(pairs, sems):
    copies = [
        pltpu.make_async_copy(source, target, sems.at[at])
        for at, (source, target) in enumerate(pairs)
    ]
    for copy in copies:
        copy.start()
    for copy in copies:
        copy.wait()


def output_kernel(*refs):
    u_refs, w_refs, outs = refs[:8], refs[8:17], refs[17:21]
    u_all, w_all, sems = refs[21:]
    z, y = lax.axis_index("z"), lax.axis_index("y")
    pairs = place_features(u_refs, u_all)
    for at, k in enumerate((0, 1, 2, 3, -1, -2, -3)):
        start = pl.multiple_of(lax.rem(z - k + 8, 8) * LANES, LANES)
        pairs.append((w_refs[at], w_all.at[pl.ds(start, LANES)]))
    far = pl.multiple_of(lax.rem(z + 4, 8) * LANES, LANES)
    half = LANES // 2
    pairs.append((w_refs[7], w_all.at[pl.ds(far, half)]))
    pairs.append((w_refs[8], w_all.at[pl.ds(pl.multiple_of(far + half, half), half)]))
    run_copies(pairs, sems)
    rows = outs[0].shape[0]
    for d, out in enumerate(outs):
        start = pl.multiple_of(lax.rem(y + d, 4) * rows, rows)
        out[...] = jnp.dot(
            u_all[pl.ds(start, rows)], w_all[...], preferred_element_type=F32
        ).astype(BF16)


def output_partials(features, weights):
    tokens, channels = features[0].shape[0], weights[0].shape[1]
    shape = jax.ShapeDtypeStruct((tokens // 4, channels), BF16)
    return pl.pallas_call(
        output_kernel,
        in_specs=[VMEM] * 17,
        out_specs=[VMEM] * 4,
        out_shape=[shape] * 4,
        scratch_shapes=[
            pltpu.VMEM((tokens, 8 * LANES), BF16),
            pltpu.VMEM((8 * LANES, channels), BF16),
            pltpu.SemaphoreType.DMA((17,)),
        ],
        name="output_partials",
        compiler_params=GRANT,
    )(*map(on_chip, (*features, *weights)))


HOPS = (3, -3, 2, -2, 1, -1, 0)


def weight_kernel(*refs):
    u_refs, m_refs, far_refs, outs = refs[:8], refs[8:12], refs[13:15], refs[15:22]
    u_all, m_all, sems = refs[22:]
    z, y = lax.axis_index("z"), lax.axis_index("y")
    pairs = place_features(u_refs, u_all)
    rows = m_refs[0].shape[0]
    for d, m_ref in enumerate(m_refs):
        start = pl.multiple_of(lax.rem(y - d + 4, 4) * rows, rows)
        pairs.append((m_ref, m_all.at[pl.ds(start, rows)]))
    run_copies(pairs, sems)

    def block(hop):
        start = pl.multiple_of(lax.rem(z + hop + 8, 8) * LANES, LANES)
        return lax.dot_general(
            u_all[:, pl.ds(start, LANES)],
            m_all[...],
            (((0,), (0,)), ((), ())),
            preferred_element_type=F32,
        ).astype(BF16)

    far = block(4)
    half = LANES // 2
    far_refs[0][...] = far[:half]
    far_refs[1][...] = far[half:]
    for out, hop in zip(outs, HOPS):
        out[...] = block(hop)


def weight_partials(features, mixed, after):
    tokens, channels = features[0].shape[0], mixed[0].shape[1]
    shape = jax.ShapeDtypeStruct((LANES, channels), BF16)
    short = jax.ShapeDtypeStruct((LANES // 2, channels), BF16)
    return pl.pallas_call(
        weight_kernel,
        in_specs=[VMEM] * 12 + [ANY],
        out_specs=[VMEM] * 9,
        out_shape=[short] * 2 + [shape] * 7,
        scratch_shapes=[
            pltpu.VMEM((tokens, 8 * LANES), BF16),
            pltpu.VMEM((tokens, channels), BF16),
            pltpu.SemaphoreType.DMA((12,)),
        ],
        name="weight_partials",
        compiler_params=GRANT,
    )(*map(on_chip, (*features, *mixed)), after)


def add_kernel(ahead_ref, behind_ref, first_ref, last_ref, ahead_out, behind_out):
    rows, half = ahead_ref.shape[0], LANES // 2
    for got, own, out, start in (
        (ahead_ref, first_ref, ahead_out, 0),
        (behind_ref, last_ref, behind_out, LANES - rows),
    ):
        if rows == half:
            other = slice(half - start, LANES - start)
            out[other] = own[other]
        span = slice(start, start + rows)
        out[span] = (got[...].astype(F32) + own[span].astype(F32)).astype(BF16)


def add_pair(ahead, behind, first, last):
    shape = jax.ShapeDtypeStruct(first.shape, BF16)
    return pl.pallas_call(
        add_kernel,
        in_specs=[VMEM] * 4,
        out_specs=[VMEM] * 2,
        out_shape=[shape] * 2,
        compiler_params=GRANT,
    )(*map(on_chip, (ahead, behind, first, last)))


def block_backward(gate, conv_input, filters, out_weight, upstream):
    rows, _ = conv_input.shape
    half = LANES // 2
    factor = (rows * SIZES["z"] * SIZES["y"]) ** (-0.5)

    ahead, behind = out_weight, out_weight
    forward, backward = [], []
    for _ in range(3):
        ahead = shift(ahead, "z", 1)
        behind = shift(behind, "z", -1)
        forward.append(ahead)
        backward.append(behind)
    weights = [out_weight] + forward + backward
    weights.append(shift(ahead[:half], "z", 1))
    weights.append(shift(behind[half:], "z", -1))

    split = jnp.moveaxis(upstream.reshape(rows, 4, LANES), 1, 0)
    own = exchanged(split, "y").reshape(4 * rows, LANES)
    near = [own] + [shift(own, "x", k) for k in (1, 2, 3)]
    features = near + [shift(near[k], "c", 1) for k in range(4)]

    prior = from_behind(conv_input[rows - TAPS :], 1)
    mixed, conv_out = conv_forward(prior, conv_input, gate, filters)
    mixed = [mixed] + [shift(mixed, "y", d) for d in (1, 2, 3)]

    partials = output_partials(features, weights)
    terms = [partials[0]] + [shift(partials[d], "y", d) for d in (1, 2, 3)]

    ahead, behind, *blocks = weight_partials(features, mixed, partials[0])
    for step in (1, 2, 3):
        ahead = shift(ahead, "z", 1)
        behind = shift(behind, "z", -1)
        pair = blocks[2 * step - 2], blocks[2 * step - 1]
        ahead, behind = add_pair(ahead, behind, *pair)
    ahead, behind = shift(ahead, "z", 1), shift(behind, "z", -1)
    summed = sum(term.astype(F32) for term in (blocks[6], ahead, behind))
    grad_weight = (summed * factor).astype(BF16)

    grad_gate, d_conv, head, local = output_gradients(
        terms, conv_out, gate, prior, conv_input
    )
    following = from_behind(head, -1)
    local = local + sum(shift(local, "y", d) for d in (1, 2, 3))
    below, above = shift(local, "z", 1), shift(local, "z", -1)
    pair = local + above
    local = pair + below
    local = local + shift(local, "z", -3) + shift(pair, "z", 3)
    grad_filter = local * factor
    grad_input = conv_backward(d_conv, following, filters)
    return (grad_gate, grad_input, grad_filter, grad_weight)


def solution(mesh):
    finer = Mesh(mesh.devices.reshape(8, 4, 4, 2), ("z", "y", "x", "c"))
    return jax.shard_map(
        block_backward,
        mesh=finer,
        in_specs=(P(SEQ, TP), P(SEQ, TP), P(TP, None), P(SEQ, TP), P(SEQ, TP)),
        out_specs=(P(SEQ, TP), P(SEQ, TP), P(TP, None), P(SEQ, TP)),
        check_vma=False,
    )
```

```python
import jax
import jax.numpy as jnp
from jax import lax
from jax.experimental import pallas as pl
from jax.experimental.pallas import tpu as pltpu
from jax.sharding import Mesh
from jax.sharding import PartitionSpec as P

GROUP = 16
TAPS = 128
LANES = 128
F32 = jnp.float32
BF16 = jnp.bfloat16
SIZES = {"z": 8, "y": 4, "x": 4, "c": 2}
SEQ = ("z", "y")
MiB = 1 << 20
SMALL = pltpu.CompilerParams(vmem_limit_bytes=10 * MiB)
LARGE = pltpu.CompilerParams(vmem_limit_bytes=16 * MiB)
TP = ("x", "c")


def shift(block, axis, distance):
    size = SIZES[axis]
    route = [(i, (i + distance) % size) for i in range(size)]
    return lax.ppermute(block, axis, route)


def exchanged(blocks, axis):
    return lax.all_to_all(blocks, axis, split_axis=0, concat_axis=0, tiled=True)


def from_behind(block, distance):
    devices = range(SIZES["z"] * SIZES["y"])
    route = [(i - distance, i) for i in devices if i - distance in devices]
    return lax.ppermute(block, SEQ, route)


def rows_and_cols():
    row = lax.broadcasted_iota(jnp.int32, (TAPS, TAPS), 0)
    col = lax.broadcasted_iota(jnp.int32, (TAPS, TAPS), 1)
    return row, col


def lane_group(shape):
    return lax.broadcasted_iota(jnp.int32, shape, len(shape) - 1) % LANES // GROUP


def pick_groups(stacked):
    lanes = lane_group((TAPS, 2 * LANES))
    out = stacked[:TAPS]
    for g in range(1, LANES // GROUP):
        out = jnp.where(lanes == g, stacked[g * TAPS : (g + 1) * TAPS], out)
    return out


STEP = 512


def for_tiles(body):
    for at in range(0, STEP, LANES):
        body(slice(at, at + LANES), slice(at // GROUP, (at + LANES) // GROUP))


def banded(rings, first):
    bands = []
    for ring in rings:
        left = jnp.where(first, ring, 0.0)
        right = jnp.where(first, 0.0, ring)
        bands.append(jnp.concatenate([left, right], axis=1).astype(BF16))
    return jnp.concatenate(bands, axis=0)


def rings_of(taps, turn):
    out = []
    for g in range(LANES // GROUP):
        wide = jnp.broadcast_to(taps[g : g + 1], (TAPS, TAPS))
        out.append(pltpu.roll(wide, turn, 1, stride=1, stride_axis=0))
    return out


def conv_kernel(prev_ref, x_ref, gate_ref, taps_ref, mixed_ref, out_ref):
    row, col = rows_and_cols()
    flip = jnp.where(row + col == TAPS - 1, 1.0, 0.0).astype(BF16)
    taps = jnp.dot(taps_ref[...], flip, preferred_element_type=F32)

    def body(at, groups):
        band = banded(rings_of(taps[groups], 1), col > row)
        x0, x1 = x_ref[:TAPS, at], x_ref[TAPS:, at]
        first = jnp.concatenate([prev_ref[:, at], x0], axis=0)
        second = jnp.concatenate([x0, x1], axis=0)
        window = jnp.concatenate([first, second], axis=1)
        conv = pick_groups(jnp.dot(band, window, preferred_element_type=F32))
        conv = jnp.concatenate([conv[:, :LANES], conv[:, LANES:]], axis=0)
        out_ref[:, at] = conv
        mixed_ref[:, at] = (gate_ref[:, at].astype(F32) * conv).astype(BF16)

    for_tiles(body)


def tile(rows):
    return pl.BlockSpec((rows, STEP), lambda i: (0, i))


def taps_tile():
    return pl.BlockSpec((STEP // GROUP, TAPS), lambda i: (i, 0))


def conv_forward(prev, x, gate, filters):
    rows, channels = x.shape
    return pl.pallas_call(
        conv_kernel,
        grid=(channels // STEP,),
        in_specs=[tile(TAPS), tile(rows), tile(rows), taps_tile()],
        out_specs=[tile(rows), tile(rows)],
        out_shape=[
            jax.ShapeDtypeStruct(x.shape, BF16),
            jax.ShapeDtypeStruct(x.shape, F32),
        ],
        name="conv_forward",
        compiler_params=SMALL,
    )(prev, x, gate, filters)


def back_kernel(d_ref, next_ref, taps_ref, out_ref):
    row, col = rows_and_cols()

    def body(at, groups):
        taps = taps_ref[groups].astype(F32)
        band = banded(rings_of(taps, 0), col >= row)
        d0, d1 = d_ref[:TAPS, at], d_ref[TAPS:, at]
        first = jnp.concatenate([d0, d1], axis=0)
        second = jnp.concatenate([d1, next_ref[:, at]], axis=0)
        window = jnp.concatenate([first, second], axis=1)
        conv = pick_groups(jnp.dot(band, window, preferred_element_type=F32))
        out_ref[:TAPS, at] = conv[:, :LANES].astype(BF16)
        out_ref[TAPS:, at] = conv[:, LANES:].astype(BF16)

    for_tiles(body)


def conv_backward(d_conv, following, filters):
    rows, channels = d_conv.shape
    return pl.pallas_call(
        back_kernel,
        grid=(channels // STEP,),
        in_specs=[tile(rows), tile(TAPS), taps_tile()],
        out_specs=tile(rows),
        out_shape=jax.ShapeDtypeStruct(d_conv.shape, BF16),
        name="conv_backward",
        compiler_params=SMALL,
    )(d_conv, following, filters)


def gradient_kernel(*refs):
    own_ref, terms, (conv_ref, gate_ref, prev_ref, x_ref) = refs[0], refs[1:5], refs[5:9]
    grad_gate_ref, d_ref, head_ref, out_ref = refs[9:]
    row, col = rows_and_cols()
    flip = jnp.where(row + col == TAPS - 1, 1.0, 0.0).astype(BF16)
    keep = col + row >= TAPS - 1

    def flipped(block):
        return jnp.dot(flip, block, preferred_element_type=F32).astype(BF16)

    blocks = flipped(prev_ref[...]), flipped(x_ref[:TAPS]), flipped(x_ref[TAPS:])

    def body(at, groups):
        prev, x0, x1 = (block[:, at] for block in blocks)
        above, below = (
            terms[k][:, at].astype(F32) + terms[k + 1][:, at].astype(F32) for k in (0, 2)
        )
        d_out = own_ref[:, at].astype(F32) + jnp.concatenate([above, below], axis=0)
        grad_gate_ref[:, at] = (d_out * conv_ref[:, at]).astype(BF16)
        d_conv = (d_out * gate_ref[:, at].astype(F32)).astype(BF16)
        d_ref[:, at] = d_conv
        head_ref[:, at] = d_conv[:TAPS]
        first = jnp.concatenate([prev, x0], axis=0)
        second = jnp.concatenate([x0, x1], axis=0)
        window = jnp.concatenate([first, second], axis=1)
        both = jnp.concatenate([d_conv[:TAPS], d_conv[TAPS:]], axis=1)
        lanes = lane_group(both.shape)
        zero = jnp.zeros_like(both)
        left = [jnp.where(lanes == g, both, zero) for g in range(LANES // GROUP)]
        left = jnp.concatenate(left, axis=0)
        table = lax.dot_general(
            left, window, (((1,), (1,)), ((), ())), preferred_element_type=F32
        )
        sums = []
        for g in range(LANES // GROUP):
            part = table[g * TAPS : (g + 1) * TAPS]
            ring = jnp.where(keep, part[:, TAPS:], part[:, :TAPS])
            ring = pltpu.roll(ring, 1, 1, stride=1, stride_axis=0)
            sums.append(jnp.sum(ring, axis=0, keepdims=True))
        out_ref[groups] = jnp.concatenate(sums, axis=0)

    for_tiles(body)


def output_gradients(own, terms, conv_out, gate, prev, x):
    rows, channels = x.shape
    return pl.pallas_call(
        gradient_kernel,
        grid=(channels // STEP,),
        in_specs=[tile(rows)] + [tile(TAPS)] * 4
        + [tile(rows)] * 2 + [tile(TAPS), tile(rows)],
        out_specs=[tile(rows), tile(rows), tile(TAPS), taps_tile()],
        out_shape=[
            jax.ShapeDtypeStruct(x.shape, BF16),
            jax.ShapeDtypeStruct(x.shape, BF16),
            jax.ShapeDtypeStruct(prev.shape, BF16),
            jax.ShapeDtypeStruct((channels // GROUP, TAPS), F32),
        ],
        name="output_gradients",
        compiler_params=SMALL,
    )(own, *terms, conv_out, gate, prev, x)


ANY = pl.BlockSpec(memory_space=pl.ANY)
VMEM = pl.BlockSpec(memory_space=pltpu.VMEM)


def on_chip(blocks):
    return [pltpu.with_memory_space_constraint(b, pltpu.VMEM) for b in blocks]


def owners():
    x, c = lax.axis_index("x"), lax.axis_index("c")
    for at in range(8):
        yield 2 * lax.rem(x - at % 4 + 4, 4) + (c if at < 4 else 1 - c)


def for_columns(body, channels):
    for at in range(0, channels, 2 * LANES):
        body(pl.ds(at, 2 * LANES))


def run_copies(pairs, sems):
    copies = [
        pltpu.make_async_copy(source, target, sems.at[at])
        for at, (source, target) in enumerate(pairs)
    ]
    for copy in copies:
        copy.start()
    for copy in copies:
        copy.wait()


def output_kernel(*refs):
    u_refs, w_refs, own_ref, outs = refs[:8], refs[8:17], refs[17], refs[18:24]
    u_all, w_all, total, sems = refs[24:]
    z, y = lax.axis_index("z"), lax.axis_index("y")
    rows = own_ref.shape[0]
    half = rows // 2
    pairs = []
    for u_ref, owner in zip(u_refs, owners()):
        lanes = pl.ds(pl.multiple_of(owner * LANES, LANES), LANES)
        pairs.append((u_ref, u_all.at[:, lanes]))
    for at, k in enumerate((0, 1, 2, 3, -1, -2, -3)):
        start = pl.multiple_of(lax.rem(z - k + 8, 8) * LANES, LANES)
        pairs.append((w_refs[at], w_all.at[pl.ds(start, LANES)]))
    far = pl.multiple_of(lax.rem(z + 4, 8) * LANES, LANES)
    later = pl.multiple_of(far + LANES // 2, LANES // 2)
    pairs.append((w_refs[7], w_all.at[pl.ds(far, LANES // 2)]))
    pairs.append((w_refs[8], w_all.at[pl.ds(later, LANES // 2)]))
    run_copies(pairs, sems)
    places = ((2, 0), (2, half), (1, half), (3, 0), (1, 0), (3, half))

    def body(lanes):
        sums = jnp.dot(u_all[...], w_all[:, lanes], preferred_element_type=F32)
        total[:, lanes] = sums.astype(BF16)

    for_columns(body, own_ref.shape[1])
    own_ref[...] = total[pl.ds(pl.multiple_of(y * rows, rows), rows)]
    for out, (d, at) in zip(outs, places):
        start = pl.multiple_of(lax.rem(y + d, 4) * rows + at, half)
        out[...] = total[pl.ds(start, half)]


def output_partials(features, weights):
    tokens, channels = features[0].shape[0], weights[0].shape[1]
    shape = jax.ShapeDtypeStruct((tokens // 4, channels), BF16)
    short = jax.ShapeDtypeStruct((tokens // 8, channels), BF16)
    return pl.pallas_call(
        output_kernel,
        in_specs=[ANY] + [VMEM] * 7 + [ANY] + [VMEM] * 8,
        out_specs=[VMEM] * 7,
        out_shape=[shape] + [short] * 6,
        scratch_shapes=[
            pltpu.VMEM((tokens, 8 * LANES), BF16),
            pltpu.VMEM((8 * LANES, channels), BF16),
            pltpu.VMEM((tokens, channels), BF16),
            pltpu.SemaphoreType.DMA((17,)),
        ],
        name="output_partials",
        compiler_params=LARGE,
    )(features[0], *on_chip(features[1:]), weights[0], *on_chip(weights[1:]))


HOPS = (3, -3, 2, -2, 1, -1, 0)


def weight_kernel(*refs):
    u_refs, m_refs, far_refs, outs = refs[:8], refs[8:12], refs[13:15], refs[15:22]
    u_all, m_all, flipped, sems = refs[22:]
    z, y = lax.axis_index("z"), lax.axis_index("y")
    pairs = []
    for u_ref, owner in zip(u_refs, owners()):
        start = pl.multiple_of(lax.rem(owner - z + 8, 8) * LANES, LANES)
        pairs.append((u_ref, u_all.at[:, pl.ds(start, LANES)]))
    rows = m_refs[0].shape[0]
    for d, m_ref in enumerate(m_refs):
        start = pl.multiple_of(lax.rem(y - d + 4, 4) * rows, rows)
        pairs.append((m_ref, m_all.at[pl.ds(start, rows)]))
    run_copies(pairs, sems)
    flipped[...] = u_all[...].T
    half = LANES // 2

    def body(lanes):
        sums = jnp.dot(flipped[...], m_all[:, lanes], preferred_element_type=F32)
        sums = sums.astype(BF16)
        far = 4 * LANES
        far_refs[0][:, lanes] = sums[far : far + half]
        far_refs[1][:, lanes] = sums[far + half : far + LANES]
        for out, hop in zip(outs, HOPS):
            start = hop % 8 * LANES
            out[:, lanes] = sums[start : start + LANES]

    for_columns(body, m_all.shape[1])


def weight_partials(features, mixed, after):
    tokens, channels = features[0].shape[0], mixed[0].shape[1]
    shape = jax.ShapeDtypeStruct((LANES, channels), BF16)
    short = jax.ShapeDtypeStruct((LANES // 2, channels), BF16)
    return pl.pallas_call(
        weight_kernel,
        in_specs=[ANY] + [VMEM] * 7 + [ANY] + [VMEM] * 3 + [ANY],
        out_specs=[VMEM] * 9,
        out_shape=[short] * 2 + [shape] * 7,
        scratch_shapes=[
            pltpu.VMEM((tokens, 8 * LANES), BF16),
            pltpu.VMEM((tokens, channels), BF16),
            pltpu.VMEM((8 * LANES, tokens), BF16),
            pltpu.SemaphoreType.DMA((12,)),
        ],
        name="weight_partials",
        compiler_params=LARGE,
    )(features[0], *on_chip(features[1:]), mixed[0], *on_chip(mixed[1:]), after)


def add_kernel(ahead_ref, behind_ref, first_ref, last_ref, ahead_out, behind_out):
    rows, half = ahead_ref.shape[0], LANES // 2
    for got, own, out, start in (
        (ahead_ref, first_ref, ahead_out, 0),
        (behind_ref, last_ref, behind_out, LANES - rows),
    ):
        if rows == half:
            other = slice(half - start, LANES - start)
            out[other] = own[other]
        span = slice(start, start + rows)
        out[span] = (got[...].astype(F32) + own[span].astype(F32)).astype(BF16)


def add_pair(ahead, behind, first, last):
    shape = jax.ShapeDtypeStruct(first.shape, BF16)
    return pl.pallas_call(
        add_kernel,
        in_specs=[VMEM] * 4,
        out_specs=[VMEM] * 2,
        out_shape=[shape] * 2,
        compiler_params=SMALL,
    )(*on_chip((ahead, behind, first, last)))


def block_backward(gate, conv_input, filters, out_weight, upstream):
    rows, _ = conv_input.shape
    half = LANES // 2
    factor = (rows * SIZES["z"] * SIZES["y"]) ** (-0.5)

    ahead, behind = out_weight, out_weight
    forward, backward = [], []
    for _ in range(3):
        ahead = shift(ahead, "z", 1)
        behind = shift(behind, "z", -1)
        forward.append(ahead)
        backward.append(behind)
    weights = [out_weight] + forward + backward
    weights.append(shift(ahead[:half], "z", 1))
    weights.append(shift(behind[half:], "z", -1))

    split = jnp.moveaxis(upstream.reshape(rows, 4, LANES), 1, 0)
    own = exchanged(split, "y").reshape(4 * rows, LANES)
    near = [own] + [shift(own, "x", k) for k in (1, 2, 3)]
    features = near + [shift(near[k], "c", 1) for k in range(4)]

    prior = from_behind(conv_input[rows - TAPS :], 1)
    mixed, conv_out = conv_forward(prior, conv_input, gate, filters)
    mixed = [mixed] + [shift(mixed, "y", d) for d in (1, 2, 3)]

    own_sum, far_top, far_low, up_low, down_top, up_top, down_low = output_partials(
        features, weights
    )
    top, low = shift(far_top, "y", 1), shift(far_low, "y", -1)
    from_below, from_above = shift(up_low, "y", 1), shift(down_top, "y", -1)
    top, low = add_pair(top, low, up_top, down_low)
    top, low = shift(top, "y", 1), shift(low, "y", -1)
    terms = top, from_above, from_below, low

    ahead, behind, *blocks = weight_partials(features, mixed, own_sum)
    for step in (1, 2, 3):
        ahead = shift(ahead, "z", 1)
        behind = shift(behind, "z", -1)
        pair = blocks[2 * step - 2], blocks[2 * step - 1]
        ahead, behind = add_pair(ahead, behind, *pair)
    ahead, behind = shift(ahead, "z", 1), shift(behind, "z", -1)
    summed = sum(term.astype(F32) for term in (blocks[6], ahead, behind))
    grad_weight = (summed * factor).astype(BF16)

    grad_gate, d_conv, head, local = output_gradients(
        own_sum, terms, conv_out, gate, prior, conv_input
    )
    following = from_behind(head, -1)
    for step in (1, 2):
        other = shift(local, "y", step)
        local = local + other
    below, above = shift(local, "z", 1), shift(local, "z", -1)
    pair = local + above
    local = pair + below
    local = local + shift(local, "z", -3) + shift(pair, "z", 3)
    grad_filter = local * factor
    grad_input = conv_backward(d_conv, following, filters)
    return (grad_gate, grad_input, grad_filter, grad_weight)


def solution(mesh):
    finer = Mesh(mesh.devices.reshape(8, 4, 4, 2), ("z", "y", "x", "c"))
    return jax.shard_map(
        block_backward,
        mesh=finer,
        in_specs=(P(SEQ, TP), P(SEQ, TP), P(TP, None), P(SEQ, TP), P(SEQ, TP)),
        out_specs=(P(SEQ, TP), P(SEQ, TP), P(TP, None), P(SEQ, TP)),
        check_vma=False,
    )
```

```python
import jax
import jax.numpy as jnp
from jax import lax
from jax.experimental import pallas as pl
from jax.experimental.pallas import tpu as pltpu
from jax.sharding import Mesh
from jax.sharding import PartitionSpec as P

GROUP = 16
TAPS = 128
LANES = 128
F32 = jnp.float32
BF16 = jnp.bfloat16
SIZES = {"z": 8, "y": 4, "x": 4, "c": 2}
SEQ = ("z", "y")
MiB = 1 << 20
SMALL = pltpu.CompilerParams(vmem_limit_bytes=10 * MiB)
LARGE = pltpu.CompilerParams(vmem_limit_bytes=16 * MiB)
TP = ("x", "c")


def shift(block, axis, distance):
    size = SIZES[axis]
    route = [(i, (i + distance) % size) for i in range(size)]
    return lax.ppermute(block, axis, route)


def exchanged(blocks, axis):
    return lax.all_to_all(blocks, axis, split_axis=0, concat_axis=0, tiled=True)


def from_behind(block, distance):
    devices = range(SIZES["z"] * SIZES["y"])
    route = [(i - distance, i) for i in devices if i - distance in devices]
    return lax.ppermute(block, SEQ, route)


def rows_and_cols():
    row = lax.broadcasted_iota(jnp.int32, (TAPS, TAPS), 0)
    col = lax.broadcasted_iota(jnp.int32, (TAPS, TAPS), 1)
    return row, col


def lane_group(shape):
    return lax.broadcasted_iota(jnp.int32, shape, len(shape) - 1) % LANES // GROUP


def pick_groups(stacked):
    lanes = lane_group((TAPS, 2 * LANES))
    out = stacked[:TAPS]
    for g in range(1, LANES // GROUP):
        out = jnp.where(lanes == g, stacked[g * TAPS : (g + 1) * TAPS], out)
    return out


STEP = 512


def for_tiles(body):
    for at in range(0, STEP, LANES):
        body(slice(at, at + LANES), slice(at // GROUP, (at + LANES) // GROUP))


def banded(rings, first):
    bands = []
    for ring in rings:
        left = jnp.where(first, ring, 0.0)
        right = jnp.where(first, 0.0, ring)
        bands.append(jnp.concatenate([left, right], axis=1).astype(BF16))
    return jnp.concatenate(bands, axis=0)


def rings_of(taps, turn):
    out = []
    for g in range(LANES // GROUP):
        wide = jnp.broadcast_to(taps[g : g + 1], (TAPS, TAPS))
        out.append(pltpu.roll(wide, turn, 1, stride=1, stride_axis=0))
    return out


def conv_kernel(prev_ref, x_ref, gate_ref, taps_ref, mixed_ref, out_ref):
    row, col = rows_and_cols()
    flip = jnp.where(row + col == TAPS - 1, 1.0, 0.0).astype(BF16)
    taps = jnp.dot(taps_ref[...], flip, preferred_element_type=F32)

    def body(at, groups):
        band = banded(rings_of(taps[groups], 1), col > row)
        x0, x1 = x_ref[:TAPS, at], x_ref[TAPS:, at]
        first = jnp.concatenate([prev_ref[:, at], x0], axis=0)
        second = jnp.concatenate([x0, x1], axis=0)
        window = jnp.concatenate([first, second], axis=1)
        conv = pick_groups(jnp.dot(band, window, preferred_element_type=F32))
        conv = jnp.concatenate([conv[:, :LANES], conv[:, LANES:]], axis=0)
        out_ref[:, at] = conv
        mixed_ref[:, at] = (gate_ref[:, at].astype(F32) * conv).astype(BF16)

    for_tiles(body)


def tile(rows):
    return pl.BlockSpec((rows, STEP), lambda i: (0, i))


def taps_tile():
    return pl.BlockSpec((STEP // GROUP, TAPS), lambda i: (i, 0))


def conv_forward(prev, x, gate, filters):
    rows, channels = x.shape
    return pl.pallas_call(
        conv_kernel,
        grid=(channels // STEP,),
        in_specs=[tile(TAPS), tile(rows), tile(rows), taps_tile()],
        out_specs=[tile(rows), tile(rows)],
        out_shape=[
            jax.ShapeDtypeStruct(x.shape, BF16),
            jax.ShapeDtypeStruct(x.shape, F32),
        ],
        name="conv_forward",
        compiler_params=SMALL,
    )(prev, x, gate, filters)


def back_kernel(d_ref, next_ref, taps_ref, out_ref):
    row, col = rows_and_cols()

    def body(at, groups):
        taps = taps_ref[groups].astype(F32)
        band = banded(rings_of(taps, 0), col >= row)
        d0, d1 = d_ref[:TAPS, at], d_ref[TAPS:, at]
        first = jnp.concatenate([d0, d1], axis=0)
        second = jnp.concatenate([d1, next_ref[:, at]], axis=0)
        window = jnp.concatenate([first, second], axis=1)
        conv = pick_groups(jnp.dot(band, window, preferred_element_type=F32))
        out_ref[:TAPS, at] = conv[:, :LANES].astype(BF16)
        out_ref[TAPS:, at] = conv[:, LANES:].astype(BF16)

    for_tiles(body)


def conv_backward(d_conv, following, filters):
    rows, channels = d_conv.shape
    return pl.pallas_call(
        back_kernel,
        grid=(channels // STEP,),
        in_specs=[tile(rows), tile(TAPS), taps_tile()],
        out_specs=tile(rows),
        out_shape=jax.ShapeDtypeStruct(d_conv.shape, BF16),
        name="conv_backward",
        compiler_params=SMALL,
    )(d_conv, following, filters)


def gradient_kernel(*refs):
    own_ref, terms, (conv_ref, gate_ref, prev_ref, x_ref) = refs[0], refs[1:5], refs[5:9]
    grad_gate_ref, d_ref, head_ref, out_ref = refs[9:]
    row, col = rows_and_cols()
    flip = jnp.where(row + col == TAPS - 1, 1.0, 0.0).astype(BF16)
    keep = col + row >= TAPS - 1

    def flipped(block):
        return jnp.dot(flip, block, preferred_element_type=F32).astype(BF16)

    blocks = flipped(prev_ref[...]), flipped(x_ref[:TAPS]), flipped(x_ref[TAPS:])

    def body(at, groups):
        prev, x0, x1 = (block[:, at] for block in blocks)
        above, below = (
            terms[k][:, at].astype(F32) + terms[k + 1][:, at].astype(F32) for k in (0, 2)
        )
        d_out = own_ref[:, at].astype(F32) + jnp.concatenate([above, below], axis=0)
        grad_gate_ref[:, at] = (d_out * conv_ref[:, at]).astype(BF16)
        d_conv = (d_out * gate_ref[:, at].astype(F32)).astype(BF16)
        d_ref[:, at] = d_conv
        head_ref[:, at] = d_conv[:TAPS]
        first = jnp.concatenate([prev, x0], axis=0)
        second = jnp.concatenate([x0, x1], axis=0)
        window = jnp.concatenate([first, second], axis=1)
        both = jnp.concatenate([d_conv[:TAPS], d_conv[TAPS:]], axis=1)
        lanes = lane_group(both.shape)
        zero = jnp.zeros_like(both)
        left = [jnp.where(lanes == g, both, zero) for g in range(LANES // GROUP)]
        left = jnp.concatenate(left, axis=0)
        table = lax.dot_general(
            left, window, (((1,), (1,)), ((), ())), preferred_element_type=F32
        )
        sums = []
        for g in range(LANES // GROUP):
            part = table[g * TAPS : (g + 1) * TAPS]
            ring = jnp.where(keep, part[:, TAPS:], part[:, :TAPS])
            ring = pltpu.roll(ring, 1, 1, stride=1, stride_axis=0)
            sums.append(jnp.sum(ring, axis=0, keepdims=True))
        out_ref[groups] = jnp.concatenate(sums, axis=0)

    for_tiles(body)


def output_gradients(own, terms, conv_out, gate, prev, x):
    rows, channels = x.shape
    return pl.pallas_call(
        gradient_kernel,
        grid=(channels // STEP,),
        in_specs=[tile(rows)] + [tile(TAPS)] * 4
        + [tile(rows)] * 2 + [tile(TAPS), tile(rows)],
        out_specs=[tile(rows), tile(rows), tile(TAPS), taps_tile()],
        out_shape=[
            jax.ShapeDtypeStruct(x.shape, BF16),
            jax.ShapeDtypeStruct(x.shape, BF16),
            jax.ShapeDtypeStruct(prev.shape, BF16),
            jax.ShapeDtypeStruct((channels // GROUP, TAPS), F32),
        ],
        name="output_gradients",
        compiler_params=SMALL,
    )(own, *terms, conv_out, gate, prev, x)


ANY = pl.BlockSpec(memory_space=pl.ANY)
VMEM = pl.BlockSpec(memory_space=pltpu.VMEM)


def on_chip(blocks):
    return [pltpu.with_memory_space_constraint(b, pltpu.VMEM) for b in blocks]


def for_columns(body, channels):
    for at in range(0, channels, 2 * LANES):
        body(pl.ds(at, 2 * LANES))


def run_copies(pairs, sems):
    copies = [
        pltpu.make_async_copy(source, target, sems.at[at])
        for at, (source, target) in enumerate(pairs)
    ]
    for copy in copies:
        copy.start()
    for copy in copies:
        copy.wait()


def output_kernel(*refs):
    u_refs, w_refs, own_ref, outs = refs[:8], refs[8:17], refs[17], refs[18:24]
    w_all, total, sems = refs[24:]
    z, y = lax.axis_index("z"), lax.axis_index("y")
    x, c = lax.axis_index("x"), lax.axis_index("c")

    def piece(k):
        owner = lax.rem(z - k + 8, 8)
        step = lax.rem(x - owner // 2 + 4, 4)
        return (step + 4 * lax.rem(owner + c, 2)) * LANES

    pairs = []
    for at, k in enumerate((0, 1, 2, 3, -1, -2, -3, 4, 4)):
        count = w_refs[at].shape[0]
        start = piece(k) + (count if at == 8 else 0)
        start = pl.multiple_of(start, count)
        pairs.append((w_refs[at], w_all.at[pl.ds(start, count)]))
    run_copies(pairs, sems)
    rows = own_ref.shape[0]
    half = rows // 2
    places = ((2, 0), (2, half), (1, half), (3, 0), (1, 0), (3, half))

    def body(lanes):
        left = jnp.concatenate([u_ref[...] for u_ref in u_refs], axis=1)
        sums = jnp.dot(left, w_all[:, lanes], preferred_element_type=F32)
        total[:, lanes] = sums.astype(BF16)

    for_columns(body, own_ref.shape[1])
    own_ref[...] = total[pl.ds(pl.multiple_of(y * rows, rows), rows)]
    for out, (d, at) in zip(outs, places):
        start = pl.multiple_of(lax.rem(y + d, 4) * rows + at, half)
        out[...] = total[pl.ds(start, half)]


def output_partials(features, weights):
    tokens, channels = features[0].shape[0], weights[0].shape[1]
    shape = jax.ShapeDtypeStruct((tokens // 4, channels), BF16)
    short = jax.ShapeDtypeStruct((tokens // 8, channels), BF16)
    stored = (0, 1, 4)
    spaces = [pltpu.HBM if at in stored else pltpu.VMEM for at in range(9)]
    blocks = map(pltpu.with_memory_space_constraint, weights, spaces)
    return pl.pallas_call(
        output_kernel,
        in_specs=[VMEM] * 8 + [ANY if at in stored else VMEM for at in range(9)],
        out_specs=[VMEM] * 7,
        out_shape=[shape] + [short] * 6,
        scratch_shapes=[
            pltpu.VMEM((8 * LANES, channels), BF16),
            pltpu.VMEM((tokens, channels), BF16),
            pltpu.SemaphoreType.DMA((9,)),
        ],
        name="output_partials",
        compiler_params=LARGE,
    )(*on_chip(features), *blocks)


HOPS = (3, -3, 2, -2, 1, -1, 0)


def weight_kernel(*refs):
    u_refs, m_refs, far_refs, outs = refs[:8], refs[8:12], refs[13:15], refs[15:22]
    flipped, total = refs[22:]
    z, y = lax.axis_index("z"), lax.axis_index("y")
    x, c = lax.axis_index("x"), lax.axis_index("c")
    rows = m_refs[0].shape[0]
    for d in range(4):
        start = pl.multiple_of(lax.rem(y - d + 4, 4) * rows, rows)
        for at, u_ref in enumerate(u_refs):
            block = u_ref[pl.ds(start, rows)]
            flipped[at * LANES : (at + 1) * LANES, d * rows : (d + 1) * rows] = block.T

    def body(lanes):
        right = jnp.concatenate([m_ref[:, lanes] for m_ref in m_refs], axis=0)
        sums = jnp.dot(flipped[...], right, preferred_element_type=F32)
        total[:, lanes] = sums.astype(BF16)

    for_columns(body, total.shape[1])

    def block(hop):
        owner = lax.rem(z + hop + 8, 8)
        step = lax.rem(x - owner // 2 + 4, 4)
        start = (step + 4 * lax.rem(owner + c, 2)) * LANES
        return total[pl.ds(pl.multiple_of(start, LANES), LANES)]

    far = block(4)
    half = LANES // 2
    far_refs[0][...] = far[:half]
    far_refs[1][...] = far[half:]
    for out, hop in zip(outs, HOPS):
        out[...] = block(hop)


def weight_partials(features, mixed, after):
    tokens, channels = features[0].shape[0], mixed[0].shape[1]
    shape = jax.ShapeDtypeStruct((LANES, channels), BF16)
    short = jax.ShapeDtypeStruct((LANES // 2, channels), BF16)
    return pl.pallas_call(
        weight_kernel,
        in_specs=[VMEM] * 12 + [ANY],
        out_specs=[VMEM] * 9,
        out_shape=[short] * 2 + [shape] * 7,
        scratch_shapes=[
            pltpu.VMEM((8 * LANES, tokens), BF16),
            pltpu.VMEM((8 * LANES, channels), BF16),
        ],
        name="weight_partials",
        compiler_params=LARGE,
    )(*on_chip(features), *on_chip(mixed), after)


def add_kernel(ahead_ref, behind_ref, first_ref, last_ref, ahead_out, behind_out):
    rows, half = ahead_ref.shape[0], LANES // 2
    for got, own, out, start in (
        (ahead_ref, first_ref, ahead_out, 0),
        (behind_ref, last_ref, behind_out, LANES - rows),
    ):
        if rows == half:
            other = slice(half - start, LANES - start)
            out[other] = own[other]
        span = slice(start, start + rows)
        out[span] = (got[...].astype(F32) + own[span].astype(F32)).astype(BF16)


def add_pair(ahead, behind, first, last):
    shape = jax.ShapeDtypeStruct(first.shape, BF16)
    return pl.pallas_call(
        add_kernel,
        in_specs=[VMEM] * 4,
        out_specs=[VMEM] * 2,
        out_shape=[shape] * 2,
        compiler_params=SMALL,
    )(*on_chip((ahead, behind, first, last)))


def block_backward(gate, conv_input, filters, out_weight, upstream):
    rows, _ = conv_input.shape
    half = LANES // 2
    factor = (rows * SIZES["z"] * SIZES["y"]) ** (-0.5)

    ahead, behind = out_weight, out_weight
    forward, backward = [], []
    for _ in range(3):
        ahead = shift(ahead, "z", 1)
        behind = shift(behind, "z", -1)
        forward.append(ahead)
        backward.append(behind)
    weights = [out_weight] + forward + backward
    weights.append(shift(ahead[:half], "z", 1))
    weights.append(shift(behind[half:], "z", -1))

    split = jnp.moveaxis(upstream.reshape(rows, 4, LANES), 1, 0)
    own = exchanged(split, "y").reshape(4 * rows, LANES)
    near = [own] + [shift(own, "x", k) for k in (1, 2, 3)]
    features = near + [shift(near[k], "c", 1) for k in range(4)]

    prior = from_behind(conv_input[rows - TAPS :], 1)
    mixed, conv_out = conv_forward(prior, conv_input, gate, filters)
    mixed = [mixed] + [shift(mixed, "y", d) for d in (1, 2, 3)]

    own_sum, far_top, far_low, up_low, down_top, up_top, down_low = output_partials(
        features, weights
    )
    top, low = shift(far_top, "y", 1), shift(far_low, "y", -1)
    from_below, from_above = shift(up_low, "y", 1), shift(down_top, "y", -1)
    top, low = add_pair(top, low, up_top, down_low)
    top, low = shift(top, "y", 1), shift(low, "y", -1)
    terms = top, from_above, from_below, low

    ahead, behind, *blocks = weight_partials(features, mixed, own_sum)
    for step in (1, 2, 3):
        ahead = shift(ahead, "z", 1)
        behind = shift(behind, "z", -1)
        pair = blocks[2 * step - 2], blocks[2 * step - 1]
        ahead, behind = add_pair(ahead, behind, *pair)
    ahead, behind = shift(ahead, "z", 1), shift(behind, "z", -1)
    summed = sum(term.astype(F32) for term in (blocks[6], ahead, behind))
    grad_weight = (summed * factor).astype(BF16)

    grad_gate, d_conv, head, local = output_gradients(
        own_sum, terms, conv_out, gate, prior, conv_input
    )
    following = from_behind(head, -1)
    for step in (1, 2):
        other = shift(local, "y", step)
        local = local + other
    below, above = shift(local, "z", 1), shift(local, "z", -1)
    pair = local + above
    local = pair + below
    nearer, farther = shift(local, "z", -3), shift(pair, "z", 3)
    grad_filter = (local + nearer + farther) * factor
    grad_input = conv_backward(d_conv, following, filters)
    return (grad_gate, grad_input, grad_filter, grad_weight)


def solution(mesh):
    finer = Mesh(mesh.devices.reshape(8, 4, 4, 2), ("z", "y", "x", "c"))
    return jax.shard_map(
        block_backward,
        mesh=finer,
        in_specs=(P(SEQ, TP), P(SEQ, TP), P(TP, None), P(SEQ, TP), P(SEQ, TP)),
        out_specs=(P(SEQ, TP), P(SEQ, TP), P(TP, None), P(SEQ, TP)),
        check_vma=False,
    )
```

```python
import jax
import jax.numpy as jnp
from jax import lax
from jax.experimental import pallas as pl
from jax.experimental.pallas import tpu as pltpu
from jax.sharding import Mesh
from jax.sharding import PartitionSpec as P

GROUP = 16
TAPS = 128
LANES = 128
F32 = jnp.float32
BF16 = jnp.bfloat16
SIZES = {"z": 8, "y": 4, "x": 4, "c": 2}
SEQ = ("z", "y")
MiB = 1 << 20
SMALL = pltpu.CompilerParams(vmem_limit_bytes=10 * MiB)
LARGE = pltpu.CompilerParams(vmem_limit_bytes=16 * MiB)
TP = ("x", "c")


def shift(block, axis, distance):
    size = SIZES[axis]
    route = [(i, (i + distance) % size) for i in range(size)]
    return lax.ppermute(block, axis, route)


def exchanged(blocks, axis):
    return lax.all_to_all(blocks, axis, split_axis=0, concat_axis=0, tiled=True)


def from_behind(block, distance):
    devices = range(SIZES["z"] * SIZES["y"])
    route = [(i - distance, i) for i in devices if i - distance in devices]
    return lax.ppermute(block, SEQ, route)


def rows_and_cols():
    row = lax.broadcasted_iota(jnp.int32, (TAPS, TAPS), 0)
    col = lax.broadcasted_iota(jnp.int32, (TAPS, TAPS), 1)
    return row, col


def lane_group(shape):
    return lax.broadcasted_iota(jnp.int32, shape, len(shape) - 1) % LANES // GROUP


def pick_groups(stacked):
    lanes = lane_group((TAPS, 2 * LANES))
    out = stacked[:TAPS]
    for g in range(1, LANES // GROUP):
        out = jnp.where(lanes == g, stacked[g * TAPS : (g + 1) * TAPS], out)
    return out


STEP = 512


def for_tiles(body):
    for at in range(0, STEP, LANES):
        body(slice(at, at + LANES), slice(at // GROUP, (at + LANES) // GROUP))


def banded(rings, first):
    bands = []
    for ring in rings:
        left = jnp.where(first, ring, 0.0)
        right = jnp.where(first, 0.0, ring)
        bands.append(jnp.concatenate([left, right], axis=1).astype(BF16))
    return jnp.concatenate(bands, axis=0)


def rings_of(taps, turn):
    out = []
    for g in range(LANES // GROUP):
        wide = jnp.broadcast_to(taps[g : g + 1], (TAPS, TAPS))
        out.append(pltpu.roll(wide, turn, 1, stride=1, stride_axis=0))
    return out


def conv_kernel(prev_ref, x_ref, gate_ref, taps_ref, mixed_ref, out_ref):
    row, col = rows_and_cols()
    flip = jnp.where(row + col == TAPS - 1, 1.0, 0.0).astype(BF16)
    taps = jnp.dot(taps_ref[...], flip, preferred_element_type=F32)

    def body(at, groups):
        band = banded(rings_of(taps[groups], 1), col > row)
        x0, x1 = x_ref[:TAPS, at], x_ref[TAPS:, at]
        first = jnp.concatenate([prev_ref[:, at], x0], axis=0)
        second = jnp.concatenate([x0, x1], axis=0)
        window = jnp.concatenate([first, second], axis=1)
        conv = pick_groups(jnp.dot(band, window, preferred_element_type=F32))
        conv = jnp.concatenate([conv[:, :LANES], conv[:, LANES:]], axis=0)
        out_ref[:, at] = conv
        mixed_ref[:, at] = (gate_ref[:, at].astype(F32) * conv).astype(BF16)

    for_tiles(body)


def tile(rows):
    return pl.BlockSpec((rows, STEP), lambda i: (0, i))


def taps_tile():
    return pl.BlockSpec((STEP // GROUP, TAPS), lambda i: (i, 0))


def conv_forward(prev, x, gate, filters):
    rows, channels = x.shape
    return pl.pallas_call(
        conv_kernel,
        grid=(channels // STEP,),
        in_specs=[tile(TAPS), tile(rows), tile(rows), taps_tile()],
        out_specs=[tile(rows), tile(rows)],
        out_shape=[
            jax.ShapeDtypeStruct(x.shape, BF16),
            jax.ShapeDtypeStruct(x.shape, F32),
        ],
        name="conv_forward",
        compiler_params=SMALL,
    )(prev, x, gate, filters)


def back_kernel(d_ref, next_ref, taps_ref, out_ref):
    row, col = rows_and_cols()

    def body(at, groups):
        taps = taps_ref[groups].astype(F32)
        band = banded(rings_of(taps, 0), col >= row)
        d0, d1 = d_ref[:TAPS, at], d_ref[TAPS:, at]
        first = jnp.concatenate([d0, d1], axis=0)
        second = jnp.concatenate([d1, next_ref[:, at]], axis=0)
        window = jnp.concatenate([first, second], axis=1)
        conv = pick_groups(jnp.dot(band, window, preferred_element_type=F32))
        out_ref[:TAPS, at] = conv[:, :LANES].astype(BF16)
        out_ref[TAPS:, at] = conv[:, LANES:].astype(BF16)

    for_tiles(body)


def conv_backward(d_conv, following, filters):
    rows, channels = d_conv.shape
    return pl.pallas_call(
        back_kernel,
        grid=(channels // STEP,),
        in_specs=[tile(rows), tile(TAPS), taps_tile()],
        out_specs=tile(rows),
        out_shape=jax.ShapeDtypeStruct(d_conv.shape, BF16),
        name="conv_backward",
        compiler_params=SMALL,
    )(d_conv, following, filters)


def gradient_kernel(*refs):
    own_ref, terms, (conv_ref, gate_ref, prev_ref, x_ref) = refs[0], refs[1:5], refs[5:9]
    grad_gate_ref, d_ref, head_ref, out_ref = refs[9:]
    row, col = rows_and_cols()
    flip = jnp.where(row + col == TAPS - 1, 1.0, 0.0).astype(BF16)
    keep = col + row >= TAPS - 1

    def flipped(block):
        return jnp.dot(flip, block, preferred_element_type=F32).astype(BF16)

    blocks = flipped(prev_ref[...]), flipped(x_ref[:TAPS]), flipped(x_ref[TAPS:])

    def body(at, groups):
        prev, x0, x1 = (block[:, at] for block in blocks)
        above, below = (
            terms[k][:, at].astype(F32) + terms[k + 1][:, at].astype(F32) for k in (0, 2)
        )
        d_out = own_ref[:, at].astype(F32) + jnp.concatenate([above, below], axis=0)
        grad_gate_ref[:, at] = (d_out * conv_ref[:, at]).astype(BF16)
        d_conv = (d_out * gate_ref[:, at].astype(F32)).astype(BF16)
        d_ref[:, at] = d_conv
        head_ref[:, at] = d_conv[:TAPS]
        first = jnp.concatenate([prev, x0], axis=0)
        second = jnp.concatenate([x0, x1], axis=0)
        window = jnp.concatenate([first, second], axis=1)
        both = jnp.concatenate([d_conv[:TAPS], d_conv[TAPS:]], axis=1)
        lanes = lane_group(both.shape)
        zero = jnp.zeros_like(both)
        left = [jnp.where(lanes == g, both, zero) for g in range(LANES // GROUP)]
        left = jnp.concatenate(left, axis=0)
        table = lax.dot_general(
            left, window, (((1,), (1,)), ((), ())), preferred_element_type=F32
        )
        sums = []
        for g in range(LANES // GROUP):
            part = table[g * TAPS : (g + 1) * TAPS]
            ring = jnp.where(keep, part[:, TAPS:], part[:, :TAPS])
            ring = pltpu.roll(ring, 1, 1, stride=1, stride_axis=0)
            sums.append(jnp.sum(ring, axis=0, keepdims=True))
        out_ref[groups] = jnp.concatenate(sums, axis=0)

    for_tiles(body)


def output_gradients(own, terms, conv_out, gate, prev, x):
    rows, channels = x.shape
    return pl.pallas_call(
        gradient_kernel,
        grid=(channels // STEP,),
        in_specs=[tile(rows)] + [tile(TAPS)] * 4
        + [tile(rows)] * 2 + [tile(TAPS), tile(rows)],
        out_specs=[tile(rows), tile(rows), tile(TAPS), taps_tile()],
        out_shape=[
            jax.ShapeDtypeStruct(x.shape, BF16),
            jax.ShapeDtypeStruct(x.shape, BF16),
            jax.ShapeDtypeStruct(prev.shape, BF16),
            jax.ShapeDtypeStruct((channels // GROUP, TAPS), F32),
        ],
        name="output_gradients",
        compiler_params=SMALL,
    )(own, *terms, conv_out, gate, prev, x)


ANY = pl.BlockSpec(memory_space=pl.ANY)
VMEM = pl.BlockSpec(memory_space=pltpu.VMEM)


def on_chip(blocks):
    return [pltpu.with_memory_space_constraint(b, pltpu.VMEM) for b in blocks]


def for_columns(body, channels):
    for at in range(0, channels, 2 * LANES):
        body(pl.ds(at, 2 * LANES))


def run_copies(pairs, sems):
    copies = [
        pltpu.make_async_copy(source, target, sems.at[at])
        for at, (source, target) in enumerate(pairs)
    ]
    for copy in copies:
        copy.start()
    for copy in copies:
        copy.wait()


def output_kernel(places, *refs):
    u_refs, w_refs, outs = refs[:8], refs[8:17], refs[17:-2]
    w_all, sems = refs[-2:]
    z, y = lax.axis_index("z"), lax.axis_index("y")
    x, c = lax.axis_index("x"), lax.axis_index("c")

    def piece(k):
        owner = lax.rem(z - k + 8, 8)
        step = lax.rem(x - owner // 2 + 4, 4)
        return (step + 4 * lax.rem(owner + c, 2)) * LANES

    pairs = []
    for at, k in enumerate((0, 1, 2, 3, -1, -2, -3, 4, 4)):
        count = w_refs[at].shape[0]
        start = piece(k) + (count if at == 8 else 0)
        start = pl.multiple_of(start, count)
        pairs.append((w_refs[at], w_all.at[pl.ds(start, count)]))
    run_copies(pairs, sems)
    rows = u_refs[0].shape[0] // 4
    ahead = []
    for d, *_ in places:
        if d not in ahead:
            ahead.append(d)
    bands = []
    for d in ahead:
        band = pl.ds(pl.multiple_of(lax.rem(y + d, 4) * rows, rows), rows)
        bands.append(jnp.concatenate([u_ref[band] for u_ref in u_refs], axis=1))
    left = jnp.concatenate(bands, axis=0)

    def body(lanes):
        sums = jnp.dot(left, w_all[:, lanes], preferred_element_type=F32)
        sums = sums.astype(BF16)
        for out, (d, first, last) in zip(outs, places):
            start = ahead.index(d) * rows
            out[:, lanes] = sums[start + first : start + last]

    for_columns(body, w_all.shape[1])


def output_partials(features, weights, places):
    channels = weights[0].shape[1]
    stored = (0, 1, 4)
    spaces = [pltpu.HBM if at in stored else pltpu.VMEM for at in range(9)]
    blocks = map(pltpu.with_memory_space_constraint, weights, spaces)

    def kernel(*refs):
        output_kernel(places, *refs)

    return pl.pallas_call(
        kernel,
        in_specs=[VMEM] * 8 + [ANY if at in stored else VMEM for at in range(9)],
        out_specs=[VMEM] * len(places),
        out_shape=[
            jax.ShapeDtypeStruct((last - first, channels), BF16)
            for _, first, last in places
        ],
        scratch_shapes=[
            pltpu.VMEM((8 * LANES, channels), BF16),
            pltpu.SemaphoreType.DMA((9,)),
        ],
        compiler_params=LARGE,
    )(*on_chip(features), *blocks)


HOPS = (3, -3, 2, -2, 1, -1, 0)


def weight_kernel(*refs):
    u_refs, m_refs, far_refs, outs = refs[:8], refs[8:12], refs[13:15], refs[15:22]
    flipped, total = refs[22:]
    z, y = lax.axis_index("z"), lax.axis_index("y")
    x, c = lax.axis_index("x"), lax.axis_index("c")
    rows = m_refs[0].shape[0]
    for d in range(4):
        start = pl.multiple_of(lax.rem(y - d + 4, 4) * rows, rows)
        for at, u_ref in enumerate(u_refs):
            block = u_ref[pl.ds(start, rows)]
            flipped[at * LANES : (at + 1) * LANES, d * rows : (d + 1) * rows] = block.T

    def body(lanes):
        right = jnp.concatenate([m_ref[:, lanes] for m_ref in m_refs], axis=0)
        sums = jnp.dot(flipped[...], right, preferred_element_type=F32)
        total[:, lanes] = sums.astype(BF16)

    for_columns(body, total.shape[1])

    def block(hop):
        owner = lax.rem(z + hop + 8, 8)
        step = lax.rem(x - owner // 2 + 4, 4)
        start = (step + 4 * lax.rem(owner + c, 2)) * LANES
        return total[pl.ds(pl.multiple_of(start, LANES), LANES)]

    far = block(4)
    half = LANES // 2
    far_refs[0][...] = far[:half]
    far_refs[1][...] = far[half:]
    for out, hop in zip(outs, HOPS):
        out[...] = block(hop)


def weight_partials(features, mixed, after):
    tokens, channels = features[0].shape[0], mixed[0].shape[1]
    shape = jax.ShapeDtypeStruct((LANES, channels), BF16)
    short = jax.ShapeDtypeStruct((LANES // 2, channels), BF16)
    return pl.pallas_call(
        weight_kernel,
        in_specs=[VMEM] * 12 + [ANY],
        out_specs=[VMEM] * 9,
        out_shape=[short] * 2 + [shape] * 7,
        scratch_shapes=[
            pltpu.VMEM((8 * LANES, tokens), BF16),
            pltpu.VMEM((8 * LANES, channels), BF16),
        ],
        name="weight_partials",
        compiler_params=LARGE,
    )(*on_chip(features), *on_chip(mixed), after)


def add_kernel(ahead_ref, behind_ref, first_ref, last_ref, ahead_out, behind_out):
    rows, half = ahead_ref.shape[0], LANES // 2
    for got, own, out, start in (
        (ahead_ref, first_ref, ahead_out, 0),
        (behind_ref, last_ref, behind_out, LANES - rows),
    ):
        if rows == half:
            other = slice(half - start, LANES - start)
            out[other] = own[other]
        span = slice(start, start + rows)
        out[span] = (got[...].astype(F32) + own[span].astype(F32)).astype(BF16)


def add_pair(ahead, behind, first, last):
    shape = jax.ShapeDtypeStruct(first.shape, BF16)
    return pl.pallas_call(
        add_kernel,
        in_specs=[VMEM] * 4,
        out_specs=[VMEM] * 2,
        out_shape=[shape] * 2,
        compiler_params=SMALL,
    )(*on_chip((ahead, behind, first, last)))


def block_backward(gate, conv_input, filters, out_weight, upstream):
    rows, _ = conv_input.shape
    half = LANES // 2
    factor = (rows * SIZES["z"] * SIZES["y"]) ** (-0.5)

    ahead, behind = out_weight, out_weight
    forward, backward = [], []
    for _ in range(3):
        ahead = shift(ahead, "z", 1)
        behind = shift(behind, "z", -1)
        forward.append(ahead)
        backward.append(behind)
    weights = [out_weight] + forward + backward
    weights.append(shift(ahead[:half], "z", 1))
    weights.append(shift(behind[half:], "z", -1))

    split = jnp.moveaxis(upstream.reshape(rows, 4, LANES), 1, 0)
    own = exchanged(split, "y").reshape(4 * rows, LANES)
    near = [own] + [shift(own, "x", k) for k in (1, 2, 3)]
    features = near + [shift(near[k], "c", 1) for k in range(4)]

    prior = from_behind(conv_input[rows - TAPS :], 1)
    mixed, conv_out = conv_forward(prior, conv_input, gate, filters)
    mixed = [mixed] + [shift(mixed, "y", d) for d in (1, 2, 3)]

    mid = rows // 2
    places = (2, 0, mid), (2, mid, rows), (1, mid, rows), (3, 0, mid)
    places += (1, 0, mid), (3, mid, rows), (0, 0, rows)
    far_top, far_low, up_low, down_top, up_top, down_low, own_sum = output_partials(
        features, weights, places
    )
    top, low = shift(far_top, "y", 1), shift(far_low, "y", -1)
    from_below, from_above = shift(up_low, "y", 1), shift(down_top, "y", -1)
    top, low = add_pair(top, low, up_top, down_low)
    top, low = shift(top, "y", 1), shift(low, "y", -1)
    terms = top, from_above, from_below, low

    ahead, behind, *blocks = weight_partials(features, mixed, own_sum)
    for step in (1, 2, 3):
        ahead = shift(ahead, "z", 1)
        behind = shift(behind, "z", -1)
        pair = blocks[2 * step - 2], blocks[2 * step - 1]
        ahead, behind = add_pair(ahead, behind, *pair)
    ahead, behind = shift(ahead, "z", 1), shift(behind, "z", -1)
    summed = sum(term.astype(F32) for term in (blocks[6], ahead, behind))
    grad_weight = (summed * factor).astype(BF16)

    grad_gate, d_conv, head, local = output_gradients(
        own_sum, terms, conv_out, gate, prior, conv_input
    )
    following = from_behind(head, -1)
    for step in (1, 2):
        other = shift(local, "y", step)
        local = local + other
    below, above = shift(local, "z", 1), shift(local, "z", -1)
    pair = local + above
    local = pair + below
    nearer, farther = shift(local, "z", -3), shift(pair, "z", 3)
    grad_filter = (local + nearer + farther) * factor
    grad_input = conv_backward(d_conv, following, filters)
    return (grad_gate, grad_input, grad_filter, grad_weight)


def solution(mesh):
    finer = Mesh(mesh.devices.reshape(8, 4, 4, 2), ("z", "y", "x", "c"))
    return jax.shard_map(
        block_backward,
        mesh=finer,
        in_specs=(P(SEQ, TP), P(SEQ, TP), P(TP, None), P(SEQ, TP), P(SEQ, TP)),
        out_specs=(P(SEQ, TP), P(SEQ, TP), P(TP, None), P(SEQ, TP)),
        check_vma=False,
    )
```
